32 devices in a mesh: rep: 8 (over z, core), seq: 4 (over y, x).
Axes of the slice: x: 2, y: 2, z: 4, core: 2. Of those that a mesh axis runs over, the one named last changes fastest.
Arguments:
- tokens_in: bfloat16 [8, 512, 1536], P('rep', 'seq'), may hold values from -6 to 6
- qkv_weight: bfloat16 [8, 1536, 1024], P('rep'), may hold values from -6 to 6
- out_cotangent: bfloat16 [8, 512, 768], P('rep', 'seq'), may hold values from -24 to 24
- step_index: int32 [1], replicated, may hold values from 0 to 1023
Outputs:
- mixed_weight: float32 [8, 1536, 1024], P('rep', 'seq')
- input_grad: bfloat16 [8, 512, 1536], P('rep', 'seq')
The draws below stay inside these ranges and needn't reach their ends.
All inputs are finite; a program needn't handle non-finite values.
Results may differ from the reference program's by a relative error of at most 0.02.
The reference program's roundings to bfloat16 on the way (of `projected`, `rounded`, `score_grad` and `proj_grad`) count: a program that leaves them out, or rounds other values in their place, can miss the bound.
Values may be sent and summed in bfloat16 or wider, within the bound.
No kernel may reach another device: no remote copies, remote signals or barrier semaphores. Data moves between devices by JAX's collectives and lax.ppermute only.
A program may use at most 64 MiB of HBM per device.

```python
import jax
import jax.numpy as jnp
from jax import lax

D = 1536
HQ = 6
DH = 128
WINDOW = 1024
QKV = 1024
SEQ_LEN = 512
REPLICAS = 8
N_REP = 8


def draw_qkv_weight(key, part):
    key_base = jax.random.fold_in(key, 0)
    weight = jax.random.truncated_normal(key_base, -6.0, 6.0, (REPLICAS, D, QKV), jnp.float32)
    return weight.astype(jnp.bfloat16)


def steps_of(rng, extent, pieces, least, top_value):
    def one(dim, parts):
        draws = jax.random.uniform(jax.random.fold_in(jax.random.fold_in(rng, 6), dim), (parts,), jnp.float32, least / len(pieces), top_value / len(pieces))
        return jnp.repeat(jnp.exp(draws), extent[dim] // parts).reshape((-1,) + (1,) * (len(extent) - dim - 1))

    level = one(*pieces[0])
    for cut in pieces[1:]:
        level = level * one(*cut)
    return level


def normal_values(stream_key, shape, width, limit, cuts=(), kind=jnp.bfloat16):
    factor_of = steps_of(stream_key, shape, cuts, -0.22, 0.18) if cuts else 1.0
    entries = jax.random.normal(stream_key, shape, jnp.float32) * width * factor_of
    return jnp.minimum(jnp.maximum(entries, -limit), limit).astype(kind)


def setup_inputs(seed: int = 0) -> dict:
    keys = jax.random.split(jax.random.key(seed), 5)
    return {
        "tokens_in": normal_values(keys[0], (REPLICAS, SEQ_LEN, D), 1.0, 6.0, ((0, 8), (1, 4))),
        "qkv_weight": draw_qkv_weight(jax.random.fold_in(keys[4], 71), 0),
        "out_cotangent": normal_values(keys[2], (REPLICAS, SEQ_LEN, HQ * DH), 4.0, 24.0, ((0, 8), (1, 4))),
        "step_index": jax.random.randint(keys[3], (1,), 0, 1024).astype(jnp.int32),
    }


learn_rate = 2.0
masked_score = -1e30


def one_replica(rows_in, weight, cotangent, rate_now):
    scale_in = D ** -0.5
    head_cols = HQ * DH
    projected = (jnp.dot(rows_in, weight, preferred_element_type=jnp.float32) * scale_in).astype(jnp.bfloat16)
    queries = projected[:, :head_cols].reshape(SEQ_LEN, HQ, DH).astype(jnp.float32)
    key_rows = projected[:, head_cols:head_cols + DH].astype(jnp.float32)
    value_rows = projected[:, head_cols + DH:].astype(jnp.float32)
    position = jnp.arange(SEQ_LEN, dtype=jnp.int32)
    spread = position[:, None] - position[None, :]
    allowed = (spread >= 0) & (spread < WINDOW)
    scores = jnp.einsum('thd,kd->htk', queries, key_rows) * (DH ** -0.5)
    scores = jnp.where(allowed[None], scores, masked_score)
    row_peak = jnp.max(scores, axis=-1, keepdims=True)
    lifted = jnp.exp(scores - row_peak)
    prob_full = lifted / jnp.sum(lifted, axis=-1, keepdims=True)
    rounded = prob_full.astype(jnp.bfloat16).astype(jnp.float32)
    attended = jnp.einsum('htk,kd->thd', rounded, value_rows)
    grads_out = cotangent.reshape(SEQ_LEN, HQ, DH).astype(jnp.float32)
    row_delta = jnp.sum(grads_out * attended, axis=-1)
    prob_grad = jnp.einsum('thd,kd->htk', grads_out, value_rows)
    score_grad = (prob_full * (prob_grad - row_delta.T[:, :, None]) * (DH ** -0.5)).astype(jnp.bfloat16).astype(jnp.float32)
    query_grad = jnp.einsum('htk,kd->thd', score_grad, key_rows).reshape(SEQ_LEN, head_cols)
    key_grad = jnp.einsum('htk,thd->kd', score_grad, queries)
    value_grad = jnp.einsum('htk,thd->kd', rounded, grads_out)
    proj_grad = jnp.concatenate([query_grad, key_grad, value_grad], axis=1).astype(jnp.bfloat16)
    input_grad = (jnp.dot(proj_grad, weight.T, preferred_element_type=jnp.float32) * scale_in).astype(jnp.bfloat16)
    param_grad = jnp.dot(rows_in.T, proj_grad, preferred_element_type=jnp.float32) * scale_in
    updated = weight.astype(jnp.float32) - rate_now * param_grad
    return updated, input_grad


def reference(tokens_in, qkv_weight, out_cotangent, step_index):
    rate_now = learn_rate * (1.0 + step_index[0].astype(jnp.float32) / 1024.0)
    updated, input_grad = lax.map(lambda triple: one_replica(triple[0], triple[1], triple[2], rate_now), (tokens_in, qkv_weight, out_cotangent))
    levels = int(N_REP).bit_length() - 1
    chosen = step_index[0] % levels
    partner = jnp.bitwise_xor(jnp.arange(REPLICAS, dtype=jnp.int32), jnp.left_shift(jnp.int32(1), chosen).astype(jnp.int32))
    mixed_weight = 0.5 * (updated + updated[partner])
    return mixed_weight, input_grad
```

```python
from functools import partial
import math

import jax
import jax.numpy as jnp
from jax import lax
from jax.experimental import pallas as pl
from jax.experimental.pallas import tpu as pltpu
from jax.sharding import PartitionSpec as P

DH = 128
WINDOW = 1024
LEARN_RATE = 2.0
MASKED = -1e30
LOG2E = 1.4426950408889634
F32 = jnp.float32
BF16 = jnp.bfloat16


def xor_pairs(size, key):
    return [(i, i ^ key) for i in range(size)]


def dot(a, b, ca, cb):
    return lax.dot_general(a, b, (((ca,), (cb,)), ((), ())), preferred_element_type=F32)


def kv_project(tokens, weight, heads_dim, scale):
    rows, width = tokens.shape
    cols = weight.shape[1] - heads_dim
    steps = 3

    def body(x_ref, w_ref, o_ref, acc):
        i = pl.program_id(0)
        part = dot(x_ref[...], w_ref[...], 1, 0)

        @pl.when(i == 0)
        def _():
            acc[...] = part

        @pl.when(i > 0)
        def _():
            acc[...] += part

        @pl.when(i == steps - 1)
        def _():
            o_ref[...] = (acc[...] * scale).astype(BF16)

    depth = width // steps
    return pl.pallas_call(
        body,
        out_shape=jax.ShapeDtypeStruct((rows, cols), BF16),
        grid=(steps,),
        in_specs=[
            pl.BlockSpec((rows, depth), lambda i: (0, i)),
            pl.BlockSpec((depth, cols), lambda i: (i, heads_dim // cols)),
        ],
        out_specs=pl.BlockSpec((rows, cols), lambda i: (0, 0)),
        scratch_shapes=[pltpu.VMEM((rows, cols), F32)],
        name="kv_project",
    )(tokens, weight)


def q_project(tokens, weight, heads_dim, scale, place, parts):
    rows, width = tokens.shape
    block = 2 * DH
    share = width // parts
    sliced = share % 128 == 0

    def body(s_ref, x_ref, w_ref, q_ref, *outs):
        q_ref[...] = (dot(x_ref[...], w_ref[...], 1, 0) * scale).astype(BF16)
        if sliced:

            @pl.when(pl.program_id(0) == 0)
            def _():
                for k, o_ref in enumerate(outs):
                    start = pl.multiple_of((s_ref[0] ^ k) * share, 128)
                    o_ref[...] = x_ref[:, pl.ds(start, share)]

    n_out = parts if sliced else 0
    res = pl.pallas_call(
        body,
        out_shape=[jax.ShapeDtypeStruct((rows, heads_dim), BF16)]
        + [jax.ShapeDtypeStruct((rows, share), BF16)] * n_out,
        grid_spec=pltpu.PrefetchScalarGridSpec(
            num_scalar_prefetch=1,
            grid=(heads_dim // block,),
            in_specs=[
                pl.BlockSpec((rows, width), lambda i, s: (0, 0)),
                pl.BlockSpec((width, block), lambda i, s: (0, i)),
            ],
            out_specs=[pl.BlockSpec((rows, block), lambda i, s: (0, i))]
            + [pl.BlockSpec((rows, share), lambda i, s: (0, 0))] * n_out,
        ),
        name="q_project",
    )(place.reshape(1), tokens, weight)
    if sliced:
        return res[0], list(res[1:])
    return res[0], [
        lax.dynamic_slice_in_dim(tokens, (place ^ k) * share, share, 1) for k in range(parts)
    ]


def attention(ids, queries, cotangent, blocks, carried, first, heads, last):
    rows = queries.shape[0]
    count = len(blocks)
    keys = count * rows
    kv = 2 * DH
    group = 2
    scale = DH ** (-0.5)
    factor = scale * LOG2E
    n_in = 3 + count + (1 if carried is not None else 0)

    def body(ids_ref, *refs):
        q_ref, g_ref = refs[0], refs[1]
        b_refs = refs[2 : 2 + count]
        c_ref = refs[2 + count] if carried is not None else None
        outs = refs[n_in - 1 :]
        dq_ref = outs[0]
        k_all = jnp.concatenate([b[:, :DH] for b in b_refs], axis=0)
        v_all = jnp.concatenate([b[:, DH:] for b in b_refs], axis=0)
        base = lax.broadcasted_iota(jnp.int32, (rows, rows), 1) - lax.broadcasted_iota(
            jnp.int32, (rows, rows), 0
        )
        bias = []
        for j in range(count):
            spread = base + (ids_ref[0] - ids_ref[1 + j]) * rows
            ok = (spread >= 0) & (spread < WINDOW) & (ids_ref[1 + j] >= 0)
            bias.append(jnp.where(ok, 0.0, MASKED))
        bias = jnp.concatenate(bias, axis=0)
        bias = jnp.concatenate([bias] * group, axis=1)
        total = None
        for h in range(0, heads, group):
            span = range(h, h + group)
            q = jnp.concatenate([q_ref[:, j * DH : (j + 1) * DH] for j in span], axis=0)
            g = jnp.concatenate([g_ref[:, j * DH : (j + 1) * DH] for j in span], axis=0)
            s = dot(k_all, q, 1, 1) + bias
            peak = jnp.max(s, axis=0, keepdims=True)
            e = jnp.exp2((s - peak) * factor)
            p = e * (1.0 / jnp.sum(e, axis=0, keepdims=True))
            r = p.astype(BF16)
            dp = dot(v_all, g, 1, 1)
            delta = jnp.sum(r.astype(F32) * dp, axis=0, keepdims=True)
            ds = (p * (dp - delta) * scale).astype(BF16)
            dq = dot(ds, k_all, 0, 0)
            for n, j in enumerate(span):
                dq_ref[:, j * DH : (j + 1) * DH] = dq[n * rows : (n + 1) * rows].astype(BF16)
            part = jnp.concatenate([dot(ds, q, 1, 0), dot(r, g, 1, 0)], axis=1)
            total = part if total is None else total + part
        if c_ref is not None:
            total = total + c_ref[...]
        if last:
            outs[1][...] = total[:rows]
            for j in range(1, count):
                outs[1 + j][...] = total[j * rows : (j + 1) * rows].astype(BF16)
        else:
            outs[1][...] = total

    cols = heads * DH
    whole = lambda shape: pl.BlockSpec(shape, lambda i, s: (0, 0))
    in_specs = [
        pl.BlockSpec((pl.Element(rows), pl.Element(cols)), lambda i, s: (0, first * DH)),
        pl.BlockSpec((pl.Element(rows), pl.Element(cols)), lambda i, s: (0, first * DH)),
    ] + [whole((rows, kv))] * count
    args = [queries, cotangent] + list(blocks)
    if carried is not None:
        in_specs.append(whole((keys, kv)))
        args.append(carried)
    if last:
        shapes = [jax.ShapeDtypeStruct((rows, kv), F32)] + [
            jax.ShapeDtypeStruct((rows, kv), BF16)
        ] * (count - 1)
    else:
        shapes = [jax.ShapeDtypeStruct((keys, kv), F32)]
    shapes = [jax.ShapeDtypeStruct((rows, cols), BF16)] + shapes
    return pl.pallas_call(
        body,
        out_shape=shapes,
        grid_spec=pltpu.PrefetchScalarGridSpec(
            num_scalar_prefetch=1,
            grid=(1,),
            in_specs=in_specs,
            out_specs=[whole(s.shape) for s in shapes],
        ),
        name="attention",
    )(ids, *args)


def update(scalars, columns, grads, weight, first, share, scale):
    cols = grads[0].shape[1]
    count = len(columns)

    def body(s_ref, *refs):
        x = jnp.concatenate([r[...] for r in refs[:count]], axis=0)
        g = jnp.concatenate([r[...] for r in refs[count : 2 * count]], axis=0)
        w_ref, u_ref, b_ref = refs[2 * count :]
        rate = LEARN_RATE * (1.0 + s_ref[1].astype(F32) / 1024.0)
        u = w_ref[...].astype(F32) - rate * (dot(x, g, 0, 0) * scale)
        u_ref[...] = u
        b_ref[...] = u.astype(BF16)

    whole = lambda a: pl.BlockSpec(a.shape, lambda i, s: (0, 0))
    return pl.pallas_call(
        body,
        out_shape=[
            jax.ShapeDtypeStruct((share, cols), F32),
            jax.ShapeDtypeStruct((share, cols), BF16),
        ],
        grid_spec=pltpu.PrefetchScalarGridSpec(
            num_scalar_prefetch=1,
            grid=(1,),
            in_specs=[whole(a) for a in columns]
            + [whole(a) for a in grads]
            + [pl.BlockSpec((pl.Element(share), pl.Element(cols)), lambda i, s: (s[0] * share, first))],
            out_specs=[pl.BlockSpec((share, cols), lambda i, s: (0, 0))] * 2,
        ),
        name="update",
    )(scalars, *columns, *grads, weight)


def average(target, updated, partner, first, width):
    share, cols = updated.shape

    def body(*refs):
        u_ref, p_ref, o_ref = refs[-3:]
        o_ref[...] = 0.5 * (u_ref[...] + p_ref[...].astype(F32))

    block = pl.BlockSpec((share, cols), lambda i: (0, 0))
    args, specs, alias = [updated, partner], [block, block], {}
    if target is not None:
        args, specs, alias = (
            [target] + args,
            [pl.BlockSpec(memory_space=pl.ANY)] + specs,
            {0: 0},
        )
    return pl.pallas_call(
        body,
        out_shape=jax.ShapeDtypeStruct((share, width), F32),
        grid=(1,),
        in_specs=specs,
        out_specs=pl.BlockSpec((pl.Element(share), pl.Element(cols)), lambda i: (0, first)),
        input_output_aliases=alias,
        name="average",
    )(*args)


def input_gradient(pieces, weight, scale):
    rows = pieces[0].shape[0]
    width, cols = weight.shape
    steps = 3
    block = width // steps

    def body(*refs):
        w_ref, o_ref = refs[-2:]
        g = jnp.concatenate([r[...] for r in refs[:-2]], axis=1)
        o_ref[...] = (dot(g, w_ref[...], 1, 1) * scale).astype(BF16)

    return pl.pallas_call(
        body,
        out_shape=jax.ShapeDtypeStruct((rows, width), BF16),
        grid=(steps,),
        in_specs=[pl.BlockSpec(p.shape, lambda i: (0, 0)) for p in pieces]
        + [pl.BlockSpec((block, cols), lambda i: (i, 0))],
        out_specs=pl.BlockSpec((rows, block), lambda i: (0, i)),
        name="input_gradient",
    )(*pieces, weight)


def step(tokens, weight, cotangent, step_index, bit):
    rows, width = tokens.shape
    heads_dim = cotangent.shape[1]
    heads = heads_dim // DH
    scale = width ** (-0.5)
    parts = lax.axis_size("seq")
    share = width // parts
    place = lax.axis_index("seq").astype(jnp.int32)
    hops = min(-(-(WINDOW + rows - 1) // rows) - 1, parts - 1)
    pairwise = hops == parts - 1 and parts & (parts - 1) == 0

    def swap(array, key):
        return lax.ppermute(array, "seq", xor_pairs(parts, key))

    def from_earlier(array, hop):
        if pairwise:
            return swap(array, hop)
        return lax.ppermute(array, "seq", [(i, i + hop) for i in range(parts - hop)])

    def from_later(array, hop):
        if pairwise:
            return swap(array, hop)
        return lax.ppermute(array, "seq", [(i + hop, i) for i in range(parts - hop)])

    def gathered(array):
        if parts <= 4:
            return [array] + [swap(array, k) for k in range(1, parts)]
        full = lax.all_gather(array, "seq", axis=0, tiled=True)
        return [full]

    def partner(array):
        pairs = xor_pairs(lax.axis_size("rep"), 1 << bit)
        return lax.ppermute(array, "rep", pairs)

    own_kv = kv_project(tokens, weight, heads_dim, scale)
    blocks = [own_kv] + [from_earlier(own_kv, k) for k in range(1, hops + 1)]
    queries, columns = q_project(tokens, weight, heads_dim, scale, place, parts)
    if parts <= 4:
        columns = [columns[0]] + [swap(columns[k], k) for k in range(1, parts)]
    else:
        stacked = tokens.reshape(rows, parts, share).transpose(1, 0, 2)
        stacked = lax.all_to_all(stacked, "seq", 0, 0, tiled=False)
        columns = [stacked.reshape(parts * rows, share)]
    hop_range = jnp.arange(hops + 1, dtype=jnp.int32)
    origin = place ^ hop_range if pairwise else place - hop_range
    ids = jnp.concatenate([place[None], origin])
    scalars = jnp.stack([place, step_index[0]])

    first_heads = 2
    dq_a, carried = attention(ids, queries, cotangent, blocks, None, 0, first_heads, False)
    grads_a = gathered(dq_a)
    rest = attention(
        ids, queries, cotangent, blocks, carried, first_heads, heads - first_heads, True
    )
    dq_b, own_pair, others = rest[0], rest[1], rest[2:]
    grads_b = gathered(dq_b)
    arrived = [from_later(others[k - 1], k) for k in range(1, hops + 1)]
    own_pair = sum((a.astype(F32) for a in arrived), own_pair).astype(BF16)
    grads_c = gathered(own_pair)
    input_grad = input_gradient([dq_a, dq_b, own_pair], weight, scale)

    cuts = [0, first_heads * DH, heads_dim]
    target = None
    for grads, first in zip((grads_a, grads_b, grads_c), cuts):
        updated, sent = update(scalars, columns, grads, weight, first, share, scale)
        other = partner(sent)
        target = average(target, updated, other, first, weight.shape[1])
    return target[None], input_grad[None]


def per_device(tokens_in, qkv_weight, out_cotangent, step_index):
    levels = lax.axis_size("rep").bit_length() - 1
    branches = [partial(step, bit=bit) for bit in range(levels)]
    return lax.switch(
        step_index[0] % levels,
        branches,
        tokens_in[0],
        qkv_weight[0],
        out_cotangent[0],
        step_index,
    )


def solution(mesh):
    return jax.shard_map(
        per_device,
        mesh=mesh,
        in_specs=(P("rep", "seq", None), P("rep", None, None), P("rep", "seq", None), P()),
        out_specs=(P("rep", "seq", None), P("rep", "seq", None)),
        check_vma=False,
    )
```

```python
import jax
import jax.numpy as jnp
from jax import lax
from jax.experimental import pallas as pl
from jax.experimental.pallas import tpu as pltpu
from jax.sharding import PartitionSpec as P


DH = 128
WINDOW = 1024
LEARN_RATE = 2.0
MASKED = -1e30
LOG2E = 1.4426950408889634
F32 = jnp.float32
BF16 = jnp.bfloat16
VMEM = pltpu.MemorySpace.VMEM
SMEM = pltpu.MemorySpace.SMEM
HBM = pltpu.MemorySpace.HBM
GRANT = 16 << 20
SPLIT = {0: (6,), 1: (4, 2), 2: (3, 1, 2)}


def xor_pairs(size, key):
    return [(i, i ^ key) for i in range(size)]


def dot(a, b, ca, cb):
    return lax.dot_general(a, b, (((ca,), (cb,)), ((), ())), preferred_element_type=F32)


def local_call(body, args, shapes, scalars=0, **kwargs):
    specs = [
        pl.BlockSpec(memory_space=SMEM if i < scalars else VMEM) for i in range(len(args))
    ]
    args = [
        a if i < scalars else pltpu.with_memory_space_constraint(a, VMEM)
        for i, a in enumerate(args)
    ]
    return pl.pallas_call(
        body,
        out_shape=[VMEM(s, d) for s, d in shapes],
        in_specs=specs,
        out_specs=[pl.BlockSpec(memory_space=VMEM)] * len(shapes),
        compiler_params=pltpu.CompilerParams(vmem_limit_bytes=GRANT),
        **kwargs,
    )(*args)


def kv_project(tokens, weight, heads_dim, scale):
    rows, width = tokens.shape
    cols = weight.shape[1] - heads_dim
    steps = 1
    depth = width // steps

    def body(x_ref, w_ref, o_ref, t_ref, held, sems):
        copies = []
        for i in range(steps):
            span = pl.ds(i * depth, depth)
            one = pltpu.make_async_copy(x_ref.at[:, span], t_ref.at[:, span], sems.at[0, i])
            two = pltpu.make_async_copy(
                w_ref.at[span, heads_dim : heads_dim + cols], held.at[span], sems.at[1, i]
            )
            one.start()
            two.start()
            copies.append((one, two))
        total = None
        for i, (one, two) in enumerate(copies):
            one.wait()
            two.wait()
            span = slice(i * depth, (i + 1) * depth)
            part = dot(t_ref[:, span], held[span, :], 1, 0)
            total = part if total is None else total + part
        o_ref[...] = (total * scale).astype(BF16)

    return pl.pallas_call(
        body,
        out_shape=[VMEM((rows, cols), BF16), VMEM((rows, width), BF16)],
        in_specs=[pl.BlockSpec(memory_space=pl.ANY)] * 2,
        out_specs=[pl.BlockSpec(memory_space=VMEM)] * 2,
        scratch_shapes=[pltpu.VMEM((width, cols), BF16), pltpu.SemaphoreType.DMA((2, steps))],
        compiler_params=pltpu.CompilerParams(vmem_limit_bytes=GRANT),
        name="kv_project",
    )(*[pltpu.with_memory_space_constraint(a, HBM) for a in (tokens, weight)])


def q_project(tokens, weight, cols, scale, place_of, slices, share):
    rows = tokens.shape[0]

    def body(x_ref, w_ref, o_ref, *outs):
        for k, t_ref in enumerate(outs):
            start = pl.multiple_of(place_of(k) * share, 128)
            t_ref[...] = x_ref[:, pl.ds(start, share)]
        o_ref[...] = (dot(x_ref[...], w_ref[:, :cols], 1, 0) * scale).astype(BF16)

    shapes = [((rows, cols), BF16)] + [((rows, share), BF16)] * slices
    return local_call(body, [tokens, weight], shapes)


def attention(place_of, queries, cotangent, blocks, carried, first, heads, last, packed):
    rows = queries.shape[0]
    count = len(blocks)
    cols = heads * DH
    kv = 2 * DH
    group = 2
    scale = DH ** (-0.5)
    factor = scale * LOG2E
    packed = packed and last
    args = [queries, cotangent] + list(blocks)
    if carried is not None:
        args.append(carried)

    def body(*refs):
        q_ref, g_ref = refs[0], refs[1]
        b_refs = refs[2 : 2 + count]
        outs = refs[len(args) :]
        k_all = jnp.concatenate([b[:, :DH] for b in b_refs], axis=0)
        v_all = jnp.concatenate([b[:, DH:] for b in b_refs], axis=0)
        base = lax.broadcasted_iota(jnp.int32, (rows, rows), 1) - lax.broadcasted_iota(
            jnp.int32, (rows, rows), 0
        )
        place = place_of(0)
        bias = []
        for j in range(count):
            origin = place_of(j)
            spread = base + (place - origin) * rows
            ok = (spread >= 0) & (spread < WINDOW) & (origin >= 0)
            bias.append(jnp.where(ok, 0.0, MASKED))
        bias = jnp.concatenate(bias, axis=0)
        total = None
        for h in range(first, first + heads, group):
            span = range(h, min(h + group, first + heads))
            q = jnp.concatenate([q_ref[:, j * DH : (j + 1) * DH] for j in span], axis=0)
            g = jnp.concatenate([g_ref[:, j * DH : (j + 1) * DH] for j in span], axis=0)
            s = dot(k_all, q, 1, 1) + jnp.concatenate([bias] * len(span), axis=1)
            peak = jnp.max(s, axis=0, keepdims=True)
            e = jnp.exp2((s - peak) * factor)
            p = e * (1.0 / jnp.sum(e, axis=0, keepdims=True))
            r = p.astype(BF16)
            dp = dot(v_all, g, 1, 1)
            delta = jnp.sum(r.astype(F32) * dp, axis=0, keepdims=True)
            ds = (p * (dp - delta) * scale).astype(BF16)
            dq = dot(ds, k_all, 0, 0).astype(BF16)
            for n, j in enumerate(span):
                at = (j - first) * DH
                piece = dq[n * rows : (n + 1) * rows]
                outs[0][:, at : at + DH] = piece
                if packed:
                    for o_ref in outs[2:]:
                        o_ref[:, at : at + DH] = piece
            part = jnp.concatenate([dot(ds, q, 1, 0), dot(r, g, 1, 0)], axis=1)
            total = part if total is None else total + part
        if carried is not None:
            total = total + refs[2 + count][...]
        if not last:
            outs[1][...] = total
        else:
            outs[1][...] = total[:rows]
            for j in range(1, count):
                part = total[j * rows : (j + 1) * rows].astype(BF16)
                if packed:
                    outs[1 + j][:, cols:] = part
                else:
                    outs[1 + j][...] = part

    shapes = [((rows, cols), BF16)]
    if not last:
        shapes.append(((count * rows, kv), F32))
    else:
        shapes.append(((rows, kv), F32))
        width = cols + kv if packed else kv
        shapes += [((rows, width), BF16)] * (count - 1)
    return local_call(body, args, shapes)


def turned(step_index, columns):
    tokens, share = sum(a.shape[0] for a in columns), columns[0].shape[1]

    def body(s_ref, *refs):
        x_ref, rate_ref = refs[-2:]
        at = 0
        for ref in refs[:-2]:
            n = ref.shape[0]
            x_ref[:, at : at + n] = ref[...].T
            at += n
        rate = LEARN_RATE * (1.0 + s_ref[0].astype(F32) / 1024.0)
        rate_ref[...] = jnp.full(rate_ref.shape, rate, F32)

    shapes = [((share, tokens), BF16), ((8, 128), F32)]
    return local_call(body, [step_index] + list(columns), shapes, scalars=1)


def update(rate, columns, grads, weight, first, share, scale):
    cols = grads[0][2]

    def body(rate_ref, x_ref, *refs):
        w_ref, u_ref, b_ref = refs[-3:]
        g = jnp.concatenate([r[:, at : at + n] for r, (_, at, n) in zip(refs, grads)], axis=0)
        start = pl.multiple_of(lax.axis_index("seq") * share, share)
        w = w_ref[pl.ds(start, share), first : first + cols].astype(F32)
        step = jnp.concatenate([rate_ref[:1, :]] * (cols // 128), axis=1)
        u = w - step * (dot(x_ref[...], g, 1, 0) * scale)
        u_ref[...] = u
        b_ref[...] = u.astype(BF16)

    return local_call(
        body,
        [rate, columns] + [a for a, _, _ in grads] + [weight],
        [((share, cols), F32), ((share, cols), BF16)],
    )


def average(target, chunks, width):
    share = chunks[0][0].shape[0]
    pieces = 3 if share % 48 == 0 else 1
    step = share // pieces
    total = sum(u.shape[1] for u, _, _ in chunks)

    def body(*refs):
        o_ref, buffer, sems = refs[-3:]
        copies = []
        at = 0
        for i, (u, _, first) in enumerate(chunks):
            u_ref, p_ref = refs[2 * i], refs[2 * i + 1]
            cols = u.shape[1]
            for n in range(pieces):
                span = slice(n * step, (n + 1) * step)
                mean = 0.5 * (u_ref[span, :] + p_ref[span, :].astype(F32))
                buffer[span, at : at + cols] = mean
                copy = pltpu.make_async_copy(
                    buffer.at[span, at : at + cols],
                    o_ref.at[span, first : first + cols],
                    sems.at[i, n],
                )
                copy.start()
                copies.append(copy)
            at += cols
        for copy in copies:
            copy.wait()

    args = [pltpu.with_memory_space_constraint(a, VMEM) for u, p, _ in chunks for a in (u, p)]
    specs = [pl.BlockSpec(memory_space=VMEM)] * len(args)
    alias = {}
    if target is not None:
        alias = {len(args): 0}
        args.append(pltpu.with_memory_space_constraint(target, HBM))
        specs.append(pl.BlockSpec(memory_space=pl.ANY))
    return pl.pallas_call(
        body,
        out_shape=HBM((share, width), F32),
        in_specs=specs,
        out_specs=pl.BlockSpec(memory_space=pl.ANY),
        scratch_shapes=[
            pltpu.VMEM((share, total), F32),
            pltpu.SemaphoreType.DMA((len(chunks), pieces)),
        ],
        input_output_aliases=alias,
        compiler_params=pltpu.CompilerParams(vmem_limit_bytes=GRANT),
    )(*args)


def marker(array):
    def body(x_ref, o_ref):
        o_ref[...] = x_ref[:8, :128].astype(F32)

    return local_call(body, [array], [((8, 128), F32)])[0]


def pair_total(own, arrived, mark):
    rows, kv = own.shape

    def body(*refs):
        total = refs[0][...]
        for ref, (_, at) in zip(refs[1:], arrived):
            total = total + ref[:, at : at + kv].astype(F32)
        refs[-1][...] = total.astype(BF16)

    args = [own] + [a for a, _ in arrived] + ([] if mark is None else [mark])
    return local_call(body, args, [((rows, kv), BF16)])[0]


def input_part(pieces, weight):
    rows, cols = pieces[0].shape[0], sum(p.shape[1] for p in pieces)

    def body(*refs):
        w_ref, o_ref = refs[-2:]
        g = jnp.concatenate([r[...] for r in refs[:-2]], axis=1)
        o_ref[...] = dot(g, w_ref[:, :cols], 1, 1)

    shapes = [((rows, weight.shape[0]), F32)]
    return local_call(body, list(pieces) + [weight], shapes)[0]


def input_gradient(part, piece, weight, scale):
    rows, cols = piece.shape
    width = weight.shape[0]

    def body(part_ref, g_ref, w_ref, o_ref, held, sem):
        total = part_ref[...] + dot(g_ref[...], w_ref[:, -cols:], 1, 1)
        held[...] = (total * scale).astype(BF16)
        copy = pltpu.make_async_copy(held, o_ref, sem)
        copy.start()
        copy.wait()

    args = [pltpu.with_memory_space_constraint(a, VMEM) for a in (part, piece, weight)]
    return pl.pallas_call(
        body,
        out_shape=HBM((rows, width), BF16),
        in_specs=[pl.BlockSpec(memory_space=VMEM)] * len(args),
        out_specs=pl.BlockSpec(memory_space=pl.ANY),
        scratch_shapes=[pltpu.VMEM((rows, width), BF16), pltpu.SemaphoreType.DMA(())],
        compiler_params=pltpu.CompilerParams(vmem_limit_bytes=GRANT),
        name="input_gradient",
    )(*args)


def step(tokens, weight, cotangent, step_index, bit):
    rows, width = tokens.shape
    heads_dim = cotangent.shape[1]
    heads = heads_dim // DH
    kv = weight.shape[1] - heads_dim
    scale = width ** (-0.5)
    parts = lax.axis_size("seq")
    share = width // parts
    hops = min(-(-(WINDOW + rows - 1) // rows) - 1, parts - 1)
    pairwise = hops == parts - 1 and parts in (2, 4) and share % 128 == 0
    others = range(1, parts)
    near = range(1, hops + 1)

    def place_of(hop):
        place = lax.axis_index("seq")
        return place ^ hop if pairwise else place - hop

    def swap(array, key):
        return lax.ppermute(array, "seq", xor_pairs(parts, key))

    def shift(array, hop):
        pairs = [(i, i + hop) for i in range(parts) if 0 <= i + hop < parts]
        return lax.ppermute(array, "seq", pairs)

    def gather(array):
        return lax.all_gather(array, "seq", axis=0, tiled=True)

    def partner(array):
        return lax.ppermute(array, "rep", xor_pairs(lax.axis_size("rep"), 1 << bit))

    def exchange(array, hop):
        return swap(array, abs(hop)) if pairwise else shift(array, hop)

    own_kv, held = kv_project(tokens, weight, heads_dim, scale)
    weight, own_kv = lax.optimization_barrier((weight, own_kv))
    blocks = [own_kv] + [exchange(own_kv, k) for k in near]
    slices = parts if pairwise else 0
    res = q_project(held, weight, heads_dim, scale, place_of, slices, share)
    queries = res[0]
    if pairwise:
        columns = [res[1]] + [swap(res[1 + k], k) for k in others]
    else:
        stacked = tokens.reshape(rows, parts, share).transpose(1, 0, 2)
        stacked = lax.all_to_all(stacked, "seq", 0, 0, tiled=False)
        columns = [stacked.reshape(parts * rows, share)]

    columns, rate = turned(step_index, columns)
    split = SPLIT[min(bit, 2)]
    if sum(split) != heads:
        split = (heads,)
    tags = "abd"[: len(split)]
    alone = len(split) == 1
    cols = [n * DH for n in split]
    pieces, grads = [], []
    carried, first = None, 0
    for tag, n in zip(tags, split):
        last = first + n == heads
        packed = pairwise and last and not alone
        res = attention(place_of, queries, cotangent, blocks, carried, first, n, last, packed)
        pieces.append(res[0])
        if last and not packed:
            partials = [exchange(res[1 + k], -k) for k in near]
            arrived = [(a, 0) for a in partials]
        if packed:
            packs = [swap(res[1 + k], k) for k in others]
            grads.append([(a, 0, n * DH) for a in [res[0]] + packs])
            arrived = [(a, n * DH) for a in packs]
        elif pairwise:
            moved = [swap(res[0], k) for k in others]
            grads.append([(a, 0, n * DH) for a in [res[0]] + moved])
        else:
            grads.append([(gather(res[0]), 0, n * DH)])
        carried, first = res[1], first + n
    own_pair = res[1]
    mark = marker(pieces[0]) if bit == 1 else None
    own_pair = pair_total(own_pair, arrived, mark)
    if pairwise:
        last = [(a, 0, kv) for a in [own_pair] + [swap(own_pair, k) for k in others]]
    else:
        last = [(gather(own_pair), 0, kv)]
    grads.append(last)
    cols.append(kv)
    part = input_part(pieces, weight)
    input_grad = input_gradient(part, own_pair, weight, scale)

    target = None
    ready = []
    first = 0
    for chunk, n, tag in zip(grads, cols, tags + "c"):
        updated, sent = update(rate, columns, chunk, weight, first, share, scale)
        ready.append((updated, partner(sent), first))
        if tag == "c" or not alone:
            target = average(target, ready, weight.shape[1])
            ready = []
        first += n
    return target[None], input_grad[None]


def per_device(tokens_in, qkv_weight, out_cotangent, step_index):
    levels = lax.axis_size("rep").bit_length() - 1

    def branch(bit):
        def run(*args):
            return step(*args, bit=bit)

        return run

    return lax.switch(
        step_index[0] % levels,
        [branch(bit) for bit in range(levels)],
        tokens_in[0],
        qkv_weight[0],
        out_cotangent[0],
        step_index,
    )


def solution(mesh):
    return jax.shard_map(
        per_device,
        mesh=mesh,
        in_specs=(P("rep", "seq", None), P("rep", None, None), P("rep", "seq", None), P()),
        out_specs=(P("rep", "seq", None), P("rep", "seq", None)),
        check_vma=False,
    )
```

```python
import jax
import jax.numpy as jnp
from jax import lax
from jax.experimental import pallas as pl
from jax.experimental.pallas import tpu as pltpu
from jax.sharding import PartitionSpec as P


DH = 128
WINDOW = 1024
LEARN_RATE = 2.0
MASKED = -1e30
LOG2E = 1.4426950408889634
F32 = jnp.float32
BF16 = jnp.bfloat16
VMEM = pltpu.MemorySpace.VMEM
SMEM = pltpu.MemorySpace.SMEM
HBM = pltpu.MemorySpace.HBM
GRANT = 16 << 20
ORDER = {0: (2, 3, 1), 1: (1, 2, 3), 2: (3, 1, 2)}
SPLIT = {0: (6,), 1: (4, 2), 2: (3, 1, 2)}


def xor_pairs(size, key):
    return [(i, i ^ key) for i in range(size)]


def dot(a, b, ca, cb):
    return lax.dot_general(a, b, (((ca,), (cb,)), ((), ())), preferred_element_type=F32)


def local_call(body, args, shapes, scalars=0, **kwargs):
    specs = [
        pl.BlockSpec(memory_space=SMEM if i < scalars else VMEM) for i in range(len(args))
    ]
    args = [
        a if i < scalars else pltpu.with_memory_space_constraint(a, VMEM)
        for i, a in enumerate(args)
    ]
    return pl.pallas_call(
        body,
        out_shape=[VMEM(s, d) for s, d in shapes],
        in_specs=specs,
        out_specs=[pl.BlockSpec(memory_space=VMEM)] * len(shapes),
        compiler_params=pltpu.CompilerParams(vmem_limit_bytes=GRANT),
        **kwargs,
    )(*args)


def kv_project(tokens, weight, heads_dim, scale):
    rows, width = tokens.shape
    cols = weight.shape[1] - heads_dim
    steps = 1
    depth = width // steps

    def body(x_ref, w_ref, o_ref, t_ref, held, sems):
        copies = []
        for i in range(steps):
            span = pl.ds(i * depth, depth)
            one = pltpu.make_async_copy(x_ref.at[:, span], t_ref.at[:, span], sems.at[0, i])
            two = pltpu.make_async_copy(
                w_ref.at[span, heads_dim : heads_dim + cols], held.at[span], sems.at[1, i]
            )
            one.start()
            two.start()
            copies.append((one, two))
        total = None
        for i, (one, two) in enumerate(copies):
            one.wait()
            two.wait()
            span = slice(i * depth, (i + 1) * depth)
            part = dot(t_ref[:, span], held[span, :], 1, 0)
            total = part if total is None else total + part
        o_ref[...] = (total * scale).astype(BF16)

    return pl.pallas_call(
        body,
        out_shape=[VMEM((rows, cols), BF16), VMEM((rows, width), BF16)],
        in_specs=[pl.BlockSpec(memory_space=pl.ANY)] * 2,
        out_specs=[pl.BlockSpec(memory_space=VMEM)] * 2,
        scratch_shapes=[pltpu.VMEM((width, cols), BF16), pltpu.SemaphoreType.DMA((2, steps))],
        compiler_params=pltpu.CompilerParams(vmem_limit_bytes=GRANT),
        name="kv_project",
    )(*[pltpu.with_memory_space_constraint(a, HBM) for a in (tokens, weight)])


def q_project(tokens, weight, cols, scale, place_of, slices, share):
    rows = tokens.shape[0]

    def body(x_ref, w_ref, o_ref, *outs):
        for k, t_ref in enumerate(outs):
            start = pl.multiple_of(place_of(k) * share, 128)
            t_ref[...] = x_ref[:, pl.ds(start, share)]
        o_ref[...] = (dot(x_ref[...], w_ref[:, :cols], 1, 0) * scale).astype(BF16)

    shapes = [((rows, cols), BF16)] + [((rows, share), BF16)] * slices
    return local_call(body, [tokens, weight], shapes)


def attention(place_of, queries, cotangent, blocks, carried, first, heads, last, packed):
    rows = queries.shape[0]
    count = len(blocks)
    cols = heads * DH
    kv = 2 * DH
    group = 6
    scale = DH ** (-0.5)
    factor = scale * LOG2E
    packed = packed and last
    args = [queries, cotangent] + list(blocks)
    if carried is not None:
        args.append(carried)

    def body(*refs):
        q_ref, g_ref = refs[0], refs[1]
        b_refs = refs[2 : 2 + count]
        outs = refs[len(args) :]
        k_all = jnp.concatenate([b[:, :DH] for b in b_refs], axis=0)
        v_all = jnp.concatenate([b[:, DH:] for b in b_refs], axis=0)
        base = lax.broadcasted_iota(jnp.int32, (rows, rows), 1) - lax.broadcasted_iota(
            jnp.int32, (rows, rows), 0
        )
        place = place_of(0)
        bias = []
        for j in range(count):
            origin = place_of(j)
            spread = base + (place - origin) * rows
            ok = (spread >= 0) & (spread < WINDOW) & (origin >= 0)
            bias.append(jnp.where(ok, 0.0, MASKED))
        bias = jnp.concatenate(bias, axis=0)
        total = None
        for h in range(first, first + heads, group):
            span = range(h, min(h + group, first + heads))
            q = jnp.concatenate([q_ref[:, j * DH : (j + 1) * DH] for j in span], axis=0)
            g = jnp.concatenate([g_ref[:, j * DH : (j + 1) * DH] for j in span], axis=0)
            s = dot(k_all, q, 1, 1) + jnp.concatenate([bias] * len(span), axis=1)
            peak = jnp.max(s, axis=0, keepdims=True)
            e = jnp.exp2((s - peak) * factor)
            p = e * (1.0 / jnp.sum(e, axis=0, keepdims=True))
            r = p.astype(BF16)
            dp = dot(v_all, g, 1, 1)
            delta = jnp.sum(r.astype(F32) * dp, axis=0, keepdims=True)
            ds = (p * (dp - delta) * scale).astype(BF16)
            dq = dot(ds, k_all, 0, 0).astype(BF16)
            for n, j in enumerate(span):
                at = (j - first) * DH
                piece = dq[n * rows : (n + 1) * rows]
                outs[0][:, at : at + DH] = piece
                if packed:
                    for o_ref in outs[2:]:
                        o_ref[:, at : at + DH] = piece
            part = jnp.concatenate([dot(ds, q, 1, 0), dot(r, g, 1, 0)], axis=1)
            total = part if total is None else total + part
        if carried is not None:
            total = total + refs[2 + count][...]
        if not last:
            outs[1][...] = total
        else:
            outs[1][...] = total[:rows]
            for j in range(1, count):
                part = total[j * rows : (j + 1) * rows].astype(BF16)
                if packed:
                    outs[1 + j][:, cols:] = part
                else:
                    outs[1 + j][...] = part

    shapes = [((rows, cols), BF16)]
    if not last:
        shapes.append(((count * rows, kv), F32))
    else:
        shapes.append(((rows, kv), F32))
        width = cols + kv if packed else kv
        shapes += [((rows, width), BF16)] * (count - 1)
    return local_call(body, args, shapes)


def turned(step_index, columns):
    tokens, share = sum(a.shape[0] for a in columns), columns[0].shape[1]

    def body(s_ref, *refs):
        x_ref, rate_ref = refs[-2:]
        at = 0
        for ref in refs[:-2]:
            n = ref.shape[0]
            x_ref[:, at : at + n] = ref[...].T
            at += n
        rate = LEARN_RATE * (1.0 + s_ref[0].astype(F32) / 1024.0)
        rate_ref[...] = jnp.full(rate_ref.shape, rate, F32)

    shapes = [((share, tokens), BF16), ((8, 128), F32)]
    return local_call(body, [step_index] + list(columns), shapes, scalars=1)


def update(rate, columns, grads, weight, first, share, scale):
    cols = grads[0][2]

    def body(rate_ref, x_ref, *refs):
        w_ref, u_ref, b_ref = refs[-3:]
        g = jnp.concatenate([r[:, at : at + n] for r, (_, at, n) in zip(refs, grads)], axis=0)
        start = pl.multiple_of(lax.axis_index("seq") * share, share)
        w = w_ref[pl.ds(start, share), first : first + cols].astype(F32)
        step = jnp.concatenate([rate_ref[:1, :]] * (cols // 128), axis=1)
        u = w - step * (dot(x_ref[...], g, 1, 0) * scale)
        u_ref[...] = u
        b_ref[...] = u.astype(BF16)

    return local_call(
        body,
        [rate, columns] + [a for a, _, _ in grads] + [weight],
        [((share, cols), F32), ((share, cols), BF16)],
    )


def average(target, chunks, width):
    share = chunks[0][0].shape[0]
    pieces = 3 if share % 48 == 0 else 1
    step = share // pieces
    total = sum(u.shape[1] for u, _, _ in chunks)

    def body(*refs):
        o_ref, buffer, sems = refs[-3:]
        copies = []
        at = 0
        for i, (u, _, first) in enumerate(chunks):
            u_ref, p_ref = refs[2 * i], refs[2 * i + 1]
            cols = u.shape[1]
            for n in range(pieces):
                span = slice(n * step, (n + 1) * step)
                mean = 0.5 * (u_ref[span, :] + p_ref[span, :].astype(F32))
                buffer[span, at : at + cols] = mean
                copy = pltpu.make_async_copy(
                    buffer.at[span, at : at + cols],
                    o_ref.at[span, first : first + cols],
                    sems.at[i, n],
                )
                copy.start()
                copies.append(copy)
            at += cols
        for copy in copies:
            copy.wait()

    args = [pltpu.with_memory_space_constraint(a, VMEM) for u, p, _ in chunks for a in (u, p)]
    specs = [pl.BlockSpec(memory_space=VMEM)] * len(args)
    alias = {}
    if target is not None:
        alias = {len(args): 0}
        args.append(pltpu.with_memory_space_constraint(target, HBM))
        specs.append(pl.BlockSpec(memory_space=pl.ANY))
    return pl.pallas_call(
        body,
        out_shape=HBM((share, width), F32),
        in_specs=specs,
        out_specs=pl.BlockSpec(memory_space=pl.ANY),
        scratch_shapes=[
            pltpu.VMEM((share, total), F32),
            pltpu.SemaphoreType.DMA((len(chunks), pieces)),
        ],
        input_output_aliases=alias,
        compiler_params=pltpu.CompilerParams(vmem_limit_bytes=GRANT),
    )(*args)


def marker(array):
    def body(x_ref, o_ref):
        o_ref[...] = x_ref[:8, :128].astype(F32)

    return local_call(body, [array], [((8, 128), F32)])[0]


def pair_total(own, arrived, mark):
    rows, kv = own.shape

    def body(*refs):
        total = refs[0][...]
        for ref, (_, at) in zip(refs[1:], arrived):
            total = total + ref[:, at : at + kv].astype(F32)
        refs[-1][...] = total.astype(BF16)

    args = [own] + [a for a, _ in arrived] + ([] if mark is None else [mark])
    return local_call(body, args, [((rows, kv), BF16)])[0]


def input_part(pieces, weight):
    rows, cols = pieces[0].shape[0], sum(p.shape[1] for p in pieces)

    def body(*refs):
        w_ref, o_ref = refs[-2:]
        g = jnp.concatenate([r[...] for r in refs[:-2]], axis=1)
        o_ref[...] = dot(g, w_ref[:, :cols], 1, 1)

    shapes = [((rows, weight.shape[0]), F32)]
    return local_call(body, list(pieces) + [weight], shapes)[0]


def input_gradient(part, piece, weight, scale):
    rows, cols = piece.shape
    width = weight.shape[0]

    def body(part_ref, g_ref, w_ref, o_ref, held, sem):
        total = part_ref[...] + dot(g_ref[...], w_ref[:, -cols:], 1, 1)
        held[...] = (total * scale).astype(BF16)
        copy = pltpu.make_async_copy(held, o_ref, sem)
        copy.start()
        copy.wait()

    args = [pltpu.with_memory_space_constraint(a, VMEM) for a in (part, piece, weight)]
    return pl.pallas_call(
        body,
        out_shape=HBM((rows, width), BF16),
        in_specs=[pl.BlockSpec(memory_space=VMEM)] * len(args),
        out_specs=pl.BlockSpec(memory_space=pl.ANY),
        scratch_shapes=[pltpu.VMEM((rows, width), BF16), pltpu.SemaphoreType.DMA(())],
        compiler_params=pltpu.CompilerParams(vmem_limit_bytes=GRANT),
        name="input_gradient",
    )(*args)


def step(tokens, weight, cotangent, step_index, bit):
    rows, width = tokens.shape
    heads_dim = cotangent.shape[1]
    heads = heads_dim // DH
    kv = weight.shape[1] - heads_dim
    scale = width ** (-0.5)
    parts = lax.axis_size("seq")
    share = width // parts
    hops = min(-(-(WINDOW + rows - 1) // rows) - 1, parts - 1)
    pairwise = hops == parts - 1 and parts in (2, 4) and share % 128 == 0
    others = [k for k in ORDER[min(bit, 2)] if k < parts] if parts <= 4 else range(1, parts)
    near = range(1, hops + 1)

    def place_of(hop):
        place = lax.axis_index("seq")
        return place ^ hop if pairwise else place - hop

    def swap(array, key):
        return lax.ppermute(array, "seq", xor_pairs(parts, key))

    def shift(array, hop):
        pairs = [(i, i + hop) for i in range(parts) if 0 <= i + hop < parts]
        return lax.ppermute(array, "seq", pairs)

    def gather(array):
        return lax.all_gather(array, "seq", axis=0, tiled=True)

    def partner(array):
        return lax.ppermute(array, "rep", xor_pairs(lax.axis_size("rep"), 1 << bit))

    def exchange(array, hop):
        return swap(array, abs(hop)) if pairwise else shift(array, hop)

    own_kv, held = kv_project(tokens, weight, heads_dim, scale)
    weight, own_kv = lax.optimization_barrier((weight, own_kv))
    blocks = [own_kv] + [exchange(own_kv, k) for k in near]
    slices = parts if pairwise else 0
    res = q_project(held, weight, heads_dim, scale, place_of, slices, share)
    queries = res[0]
    if pairwise:
        columns = [res[1]] + [swap(res[1 + k], k) for k in others]
    else:
        stacked = tokens.reshape(rows, parts, share).transpose(1, 0, 2)
        stacked = lax.all_to_all(stacked, "seq", 0, 0, tiled=False)
        columns = [stacked.reshape(parts * rows, share)]

    columns, rate = turned(step_index, columns)
    split = SPLIT[min(bit, 2)]
    if sum(split) != heads:
        split = (heads,)
    tags = "abd"[: len(split)]
    alone = len(split) == 1
    cols = [n * DH for n in split]
    pieces, grads = [], []
    carried, first = None, 0
    for tag, n in zip(tags, split):
        last = first + n == heads
        packed = pairwise and last and not alone
        res = attention(place_of, queries, cotangent, blocks, carried, first, n, last, packed)
        pieces.append(res[0])
        if last and not packed:
            partials = [exchange(res[1 + k], -k) for k in near]
            arrived = [(a, 0) for a in partials]
        if packed:
            packs = [swap(res[1 + k], k) for k in others]
            grads.append([(a, 0, n * DH) for a in [res[0]] + packs])
            arrived = [(a, n * DH) for a in packs]
        elif pairwise:
            moved = [swap(res[0], k) for k in others]
            grads.append([(a, 0, n * DH) for a in [res[0]] + moved])
        else:
            grads.append([(gather(res[0]), 0, n * DH)])
        carried, first = res[1], first + n
    own_pair = res[1]
    mark = marker(pieces[0]) if bit == 1 else None
    own_pair = pair_total(own_pair, arrived, mark)
    if pairwise:
        last = [(a, 0, kv) for a in [own_pair] + [swap(own_pair, k) for k in others]]
    else:
        last = [(gather(own_pair), 0, kv)]
    grads.append(last)
    cols.append(kv)
    part = input_part(pieces, weight)
    input_grad = input_gradient(part, own_pair, weight, scale)

    target = None
    ready = []
    first = 0
    for chunk, n, tag in zip(grads, cols, tags + "c"):
        updated, sent = update(rate, columns, chunk, weight, first, share, scale)
        ready.append((updated, partner(sent), first))
        if tag == "c" or not alone:
            target = average(target, ready, weight.shape[1])
            ready = []
        first += n
    return target[None], input_grad[None]


def per_device(tokens_in, qkv_weight, out_cotangent, step_index):
    levels = lax.axis_size("rep").bit_length() - 1

    def branch(bit):
        def run(*args):
            return step(*args, bit=bit)

        return run

    return lax.switch(
        step_index[0] % levels,
        [branch(bit) for bit in range(levels)],
        tokens_in[0],
        qkv_weight[0],
        out_cotangent[0],
        step_index,
    )


def solution(mesh):
    return jax.shard_map(
        per_device,
        mesh=mesh,
        in_specs=(P("rep", "seq", None), P("rep", None, None), P("rep", "seq", None), P()),
        out_specs=(P("rep", "seq", None), P("rep", "seq", None)),
        check_vma=False,
    )
```
